32 devices in a mesh: expert: 16 (over z, x, core), tensor: 2 (over y).
Axes of the slice: x: 2, y: 2, z: 4, core: 2. Of those that a mesh axis runs over, the one named last changes fastest.
Arguments:
- grad_out: bfloat16 [2048, 4096], P('expert', 'tensor'), may hold values from -1 to 1
- routes: int32 [2048, 6], P('expert'), may hold values from 0 to 15, all different within a row; in each aligned block of 128 rows (0 to 127, 128 to 255, ...) at most 96 rows name the same one
- scores: float32 [2048, 6], P('expert'), may hold values from -6 to 6
- hidden_act: bfloat16 [16, 1536, 1408], P('expert', None, 'tensor'), may hold values from -6 to 6
- w_down: bfloat16 [16, 1408, 4096], P('expert', 'tensor'), may hold values from -0.15625 to 0.15625
Outputs:
- d_hidden: bfloat16 [16, 1536, 1408], P('expert', None, 'tensor')
- grad_w: bfloat16 [16, 1408, 4096], P('expert', 'tensor')
- grad_scores: float32 [2048, 6], P('expert')
The draws below stay inside these ranges and needn't reach their ends.
Inputs may be any that keep to these rules, and one draw needn't show every extreme that they name: `routes`: each row names 6 different experts. In each aligned block of 128 rows no expert is named by more than 96 rows, a bound that some block reaches.
All inputs are finite; a program needn't handle non-finite values.
Results may differ from the reference program's by a relative error of at most 0.012.
Values may be sent and summed in bfloat16 or wider, within the bound.
A program may use at most 128 MiB of HBM per device.

```python
import math
import jax
import jax.numpy as jnp
import numpy as np
from jax import lax

D = 4096
FF = 1408
TOP = 6
TOK_DEV = 128
EXPERTS = 16
MOST = 96
CAP = 1536
TOKENS = 2048
N_EXPERT = 16


def block_scale(rng, extent, shards, low, largest):
    def one(dim, shards_of):
        steps = jax.random.uniform(jax.random.fold_in(jax.random.fold_in(rng, 6), dim), (shards_of,), jnp.float32, low / len(shards), largest / len(shards))
        return jnp.repeat(jnp.exp(steps), extent[dim] // shards_of).reshape((-1,) + (1,) * (len(extent) - dim - 1))

    loudness = one(*shards[0])
    for cut in shards[1:]:
        loudness = loudness * one(*cut)
    return loudness


def shared_out(stream_key, own, number, rows, number_of, top, limit, slope):
    sequence = jax.random.permutation(stream_key, number_of)
    heavy_load, ordinary = shares(number_of, rows * top, limit, slope, True), shares(number_of, rows * top, limit, slope, False)
    places = jnp.arange(number_of)

    def named(lengths, rotation):
        used = int((lengths > 0).sum())
        fixed = max(1, used // 4)
        moved = fixed + (places - fixed + rotation * (used - fixed)) % max(1, number_of - fixed)
        return jnp.zeros((number_of,), jnp.int32).at[sequence[jnp.where(places < fixed, places, moved)]].set(jnp.asarray(lengths, jnp.int32))

    lengths = jnp.where(number % 4 == 0, named(heavy_load, number // 4), named(ordinary, number - number // 4 - 1))
    mixed = jax.random.permutation(jax.random.fold_in(own, 3), number_of)
    source_of, taker = mixed[0:number_of // 2 * 2:2], mixed[1:number_of // 2 * 2:2]
    margin = jnp.minimum(lengths[source_of] - 1, limit - lengths[taker]) // 2
    margin = jnp.where((source_of == sequence[0]) | (taker == sequence[0]) | (lengths[taker] == 0), 0, jnp.maximum(margin, 0))
    moved = jax.random.randint(jax.random.fold_in(own, 4), (number_of // 2,), 0, 1 << 20) % (margin + 1)
    lengths = lengths.at[source_of].add(-moved).at[taker].add(moved)
    items = jnp.searchsorted(jnp.cumsum(lengths), jnp.arange(rows * top), side="right").astype(jnp.int32)
    listing = items.reshape(top, rows).T
    listing = listing[jax.random.permutation(jax.random.fold_in(own, 1), rows)]
    rotation = jax.random.randint(jax.random.fold_in(own, 2), (rows, 1), 0, top)
    return jnp.take_along_axis(listing, (jnp.arange(top)[None, :] + rotation) % top, axis=1)


def shares(count, total, limit, skew, full):
    weights = [(1 << 20) // math.isqrt(grade ** skew) + 1 for grade in range(1, count + 1)]
    largest = limit if full else min(limit, max(-(-total // count), total * weights[0] // sum(weights)))
    least = 1 if total - largest >= count - 1 else 0
    counts, rest = [largest] + [least] * (count - 1), total - largest - least * (count - 1)
    while rest > 0:
        free = [i for i in range(1, count) if counts[i] < largest] or [i for i in range(1, count) if counts[i] < limit]
        mass, remaining = sum([weights[i] for i in free]), rest
        for i in free:
            more = min(limit - counts[i], max(1, remaining * weights[i] // mass), rest)
            counts[i] = counts[i] + more
            rest = rest - more
    return np.array(counts)


def gaussian(own_key, shape, width, most, split=(), kind=jnp.bfloat16):
    values = jax.random.normal(own_key, shape, jnp.float32) * width
    if len(split) > 0:
        values = block_scale(own_key, shape, split, -0.22, 0.18) * values
    return jnp.clip(values, min=-most, max=most).astype(kind)


def setup_inputs(seed: int = 0) -> dict:
    key_of = jax.random.split(jax.random.key(seed), 6)
    grad_out = gaussian(key_of[0], (TOKENS, D), 0.0625, 1.0, ((0, 16), (1, 2)))
    routes_keys = jax.random.split(jax.random.fold_in(key_of[1], 1), TOKENS // TOK_DEV)
    routes_turns = jax.random.permutation(jax.random.fold_in(key_of[1], 3), TOKENS // TOK_DEV)
    routes = jax.vmap(lambda own, number: shared_out(jax.random.fold_in(key_of[1], 2), own, number, TOK_DEV, EXPERTS, TOP, MOST, 2))(routes_keys, routes_turns).reshape((TOKENS, TOP))
    scores = gaussian(key_of[2], (TOKENS, TOP), 1.5, 6.0, ((0, 16),), jnp.float32)
    hidden_act = gaussian(key_of[3], (EXPERTS, CAP, FF), 1.0, 6.0, ((0, 16), (2, 2)))
    w_down = gaussian(key_of[4], (EXPERTS, FF, D), FF ** -0.5, 0.15625, ((0, 16), (1, 2)))
    return {"grad_out": grad_out, "routes": routes, "scores": scores, "hidden_act": hidden_act, "w_down": w_down}


def slot_places(routes):
    grouped = routes.reshape(N_EXPERT, TOK_DEV * TOP)
    onehot = (grouped[:, :, None] == jnp.arange(EXPERTS, dtype=jnp.int32)[None, None, :]).astype(jnp.int32)
    earlier = jnp.cumsum(onehot, axis=1) - onehot
    slot_rank = jnp.sum(earlier * onehot, axis=2).astype(jnp.int32)
    groups = jnp.arange(N_EXPERT, dtype=jnp.int32)[:, None]
    slots = groups * MOST + slot_rank
    return (grouped * CAP + slots).reshape(-1).astype(jnp.int32)


def reference(grad_out, routes, scores, hidden_act, w_down):
    slot_place = slot_places(routes)
    gates = jax.nn.sigmoid(scores)
    gate_sum = jnp.sum(gates, axis=1, keepdims=True)
    probs = gates / gate_sum
    token_ids = (jnp.arange(TOKENS * TOP, dtype=jnp.int32) // TOP).astype(jnp.int32)
    slot_owner = jnp.full((EXPERTS * CAP,), TOKENS, jnp.int32).at[slot_place].set(token_ids).reshape(EXPERTS, CAP)
    slot_probs = jnp.zeros((EXPERTS * CAP,), jnp.float32).at[slot_place].set(probs.reshape(-1)).reshape(EXPERTS, CAP)

    def expert(inputs):
        owners, slot_weight, saved_act, down_rows = inputs
        dispatched = jnp.take(grad_out, owners, axis=0, mode="fill", fill_value=0)
        back_proj = lax.dot_general(dispatched, down_rows, (((1,), (1,)), ((), ())), preferred_element_type=jnp.float32)
        slot_grad = jnp.sum(back_proj * saved_act.astype(jnp.float32), axis=1)
        hidden_grad = (slot_weight[:, None] * back_proj).astype(jnp.bfloat16)
        scaled = (dispatched * slot_weight[:, None]).astype(jnp.bfloat16)
        weight_grad = lax.dot_general(saved_act, scaled, (((0,), (0,)), ((), ())), preferred_element_type=jnp.float32)
        return hidden_grad, weight_grad.astype(jnp.bfloat16), slot_grad

    d_hidden, grad_w, slot_grads = lax.map(expert, (slot_owner, slot_probs, hidden_act, w_down))
    prob_grad = slot_grads.reshape(-1)[slot_place].reshape(TOKENS, TOP)
    mean_term = jnp.sum(probs * prob_grad, axis=1, keepdims=True)
    grad_scores = gates * (1.0 - gates) * (prob_grad - mean_term) / gate_sum
    return d_hidden, grad_w, grad_scores
```

```python
import functools

import jax
import jax.numpy as jnp
from jax import lax
from jax.experimental import pallas as pl
from jax.experimental.pallas import tpu as pltpu
from jax.sharding import PartitionSpec as P

MESH = pl.DeviceIdType.MESH
NT = (((1,), (1,)), ((), ()))
TN = (((0,), (0,)), ((), ()))
VMEM_BYTES = 67_000_000


def item_order(ranks):
    items = [(k, a, b) for k in range(ranks) for a in (0, 1) for b in (0, 1)]
    return sorted(items, key=lambda i: (i[0] + i[1] * 0.9 + i[2] * (1.2 + 0.5 * i[0] + 0.3 * i[1]), i))


def kernel(
    dims,
    pm_ref,
    g_ref,
    h_ref,
    w_ref,
    dh_ref,
    gw_ref,
    pd_ref,
    G,
    W,
    H,
    HT,
    HpT,
    sel,
    acc,
    obuf,
    dhb,
    bpt,
    pr,
    pgs,
    pgr,
    rs,
    sa,
    sb,
    sz,
    sp,
    pss,
    prs,
    gss,
    grs,
    ls,
    os_,
    ds_,
):
    nz, tok, feat, hid, slots = dims
    n_exp = nz * 4
    group = 4 * tok
    quarter = tok // 4
    pieces = ((0, tok - quarter, 1), (tok - quarter, quarter, 2))
    e = lax.axis_index("expert")
    y = lax.axis_index("tensor")
    z, x, c = e // 4, (e // 2) % 2, e % 2

    tables = [sorted(range(nz), key=lambda o: (abs(o - i), o)) for i in range(nz)]

    def ranked(k):
        val = jnp.int32(0)
        for i in range(nz):
            val = val + jnp.where(z == i, jnp.int32(tables[i][k]), jnp.int32(0))
        return val

    zk = [ranked(k) for k in range(nz)]

    def dev(z_, x_, y_, c_):
        return ((z_ * 2 + x_) * 2 + c_, y_)

    load_g = pltpu.make_async_copy(g_ref, G.at[z, y, pl.ds((x * 2 + c) * tok, tok), :], ls.at[0])
    load_h = pltpu.make_async_copy(h_ref, H, ls.at[1])
    load_w = pltpu.make_async_copy(w_ref, W, ls.at[2])
    load_g.start()
    load_h.start()
    load_w.start()

    barrier = pltpu.get_barrier_semaphore()
    total = n_exp * 2
    lin = e * 2 + y

    def greet(i, carry):
        to = (lin + i) % total
        pl.semaphore_signal(barrier, inc=1, device_id=(to // 2, to % 2), device_id_type=MESH)
        return carry

    lax.fori_loop(1, total, greet, 0)
    pl.semaphore_wait(barrier, total - 1)

    partner = dev(z, x, y, 1 - c)
    a_dev = dev(z, (x + 1 - c) % 2, (y + c) % 2, c)
    b_dev = dev(z, (x + c) % 2, (y + 1 - c) % 2, c)
    up_dev = dev(jnp.minimum(z + 1, nz - 1), x, y, c)
    down_dev = dev(jnp.maximum(z - 1, 0), x, y, c)

    def place(k, a, b, color, piece):
        fx = a * (1 - color) + b * color
        fy = a * color + b * (1 - color)
        x_, y_ = (x + fx) % 2, (y + fy) % 2
        row, rows, _ = pieces[piece]
        ref = G.at[zk[k], y_, pl.ds((x_ * 2 + color) * tok + row, rows), :]
        return ref, rs.at[zk[k], x_ * 2 + color, y_, piece]

    def send(ref, recv, sem, to):
        pltpu.make_async_remote_copy(ref, ref, sem, recv, device_id=to, device_id_type=MESH).start()

    def await_piece(ref, recv):
        pltpu.make_async_remote_copy(ref, ref, sp, recv, device_id=partner, device_id_type=MESH).wait_recv()

    def handle(k, a, b):
        for piece in range(len(pieces)):
            kind = pieces[piece][2]
            ref, recv = place(k, a, b, c, piece)
            if (k, a, b) != (0, 0, 0):
                await_piece(ref, recv)
            if (a, b) == (0, 0) or kind == 2:

                @pl.when(jnp.logical_and(zk[k] <= z, z < nz - 1))
                def _():
                    send(ref, recv, sz.at[0, zk[k]], up_dev)

                @pl.when(jnp.logical_and(zk[k] >= z, z > 0))
                def _():
                    send(ref, recv, sz.at[1, zk[k]], down_dev)

            if (a, b) == (0, 0) and (kind == 1 or k == 0):
                send(ref, recv, sa, a_dev)
            if b == 0 and (kind == 1 or k == 0):
                send(ref, recv, sb, b_dev)
            send(ref, recv, sp, partner)

    load_g.wait()
    handle(0, 0, 0)

    def send_p(i, carry):
        to = (e + i) % n_exp
        pltpu.make_async_remote_copy(
            pm_ref.at[to], pr.at[e], pss.at[to], prs.at[e], device_id=(to, y), device_id_type=MESH
        ).start()
        return carry

    lax.fori_loop(1, n_exp, send_p, 0)
    pr[e] = pm_ref[e]

    def wait_p(i, carry):
        frm = (e + i) % n_exp
        copy = pltpu.make_async_remote_copy(
            pm_ref.at[frm], pr.at[frm], pss.at[frm], prs.at[frm], device_id=(frm, y), device_id_type=MESH
        )
        copy.wait_recv()
        copy.wait_send()
        return carry

    lax.fori_loop(1, n_exp, wait_p, 0)
    load_h.wait()
    before = (
        lax.broadcasted_iota(jnp.int32, (tok, tok), 0) < lax.broadcasted_iota(jnp.int32, (tok, tok), 1)
    ).astype(jnp.bfloat16)
    slot_ids = lax.broadcasted_iota(jnp.int32, (slots, tok), 0).astype(jnp.float32)

    def prepare(line, carry):
        for j in range(4):
            p = pr[line * 4 + j]
            routed = (p > 0.0).astype(jnp.float32)
            rank = jnp.dot(routed.astype(jnp.bfloat16), before, preferred_element_type=jnp.float32)
            rank = jnp.where(p > 0.0, rank, -1.0)
            pick = (slot_ids == rank[0:1, :]).astype(jnp.float32).astype(jnp.bfloat16)
            sel[line * 4 + j] = pick
            rows = H[pl.ds(pl.multiple_of((line * 4 + j) * slots, 16), slots), :]
            ht = lax.dot_general(rows, pick, TN, preferred_element_type=jnp.float32)
            HT[line, :, j * tok : (j + 1) * tok] = ht.astype(jnp.bfloat16)
            HpT[line, :, j * tok : (j + 1) * tok] = (ht * p[0:1, :]).astype(jnp.bfloat16)
        return carry

    lax.fori_loop(0, nz, prepare, 0)

    def await_partner(k):
        for a in (0, 1):
            for b in (0, 1):
                for piece in range(len(pieces)):
                    await_piece(*place(k, a, b, 1 - c, piece))

    def project(k, half):
        line = zk[k]
        cols = slice(half * 2 * tok, (half + 1) * 2 * tok)
        bpt[...] = lax.dot_general(
            W[:, :feat], G[line, 0, cols, :], NT, preferred_element_type=jnp.float32
        ) + lax.dot_general(W[:, feat:], G[line, 1, cols, :], NT, preferred_element_type=jnp.float32)
        for i in range(2):
            j = half * 2 + i
            block = line * 4 + j
            back = bpt[:, i * tok : (i + 1) * tok]
            value = jnp.sum(
                back * HT[line, :, j * tok : (j + 1) * tok].astype(jnp.float32), axis=0, keepdims=True
            )
            pgs[block] = jnp.broadcast_to(value, (8, tok))
            scaled = (back * pr[block][0:1, :]).astype(jnp.bfloat16)
            dhb[pl.ds(pl.multiple_of(block * slots, 16), slots), :] = lax.dot_general(
                sel[block], scaled, NT, preferred_element_type=jnp.float32
            ).astype(jnp.bfloat16)

    def send_values(k):
        line = zk[k]
        for j in range(4):
            block = line * 4 + j
            for y_ in range(2):

                @pl.when(jnp.logical_or(block != e, y != y_))
                def _():
                    pltpu.make_async_remote_copy(
                        pgs.at[block],
                        pgr.at[y, e],
                        gss.at[y_, block],
                        grs.at[y, e],
                        device_id=(block, y_),
                        device_id_type=MESH,
                    ).start()

        rows = pl.ds(pl.multiple_of(line * 4 * slots, 16), 4 * slots)
        pltpu.make_async_copy(dhb.at[rows, :], dh_ref.at[rows, :], ds_.at[k]).start()

    width = feat // 4

    def weigh(k, half):
        line = zk[k]

        def one(n, carry):
            cols = pl.ds(pl.multiple_of(n * width, width), width)
            dest = pl.ds(pl.multiple_of(half * feat + n * width, width), width)
            part = jnp.dot(HpT[line], G[line, half, :, cols], preferred_element_type=jnp.float32)
            if k == 0:
                acc[:, dest] = part
            elif k < nz - 1:
                acc[:, dest] += part
            else:
                obuf[:, dest] = (acc[:, dest] + part).astype(jnp.bfloat16)
                pltpu.make_async_copy(obuf.at[:, dest], gw_ref.at[:, dest], os_.at[half * 4 + n]).start()
            return carry

        lax.fori_loop(0, 4, one, 0)

    units = []
    for k in range(nz):
        units.append((k, lambda k=k: (await_partner(k), project(k, 0))))
        units.append((k, lambda k=k: (project(k, 1), send_values(k))))
        units.append((k, lambda k=k: weigh(k, 0)))
        units.append((k, lambda k=k: weigh(k, 1)))

    order = item_order(nz)[1:]
    done = {k: 1 if k == 0 else 0 for k in range(nz)}
    started = False
    for item in order:
        handle(*item)
        done[item[0]] += 1
        if units and done[units[0][0]] == 4:
            if not started:
                load_w.wait()
                started = True
            units.pop(0)[1]()
    for _, unit in units:
        unit()

    pgr[y, e] = pgs[e]

    def settle(i, carry):
        at = (lin + i) % total
        e_, y_ = at // 2, at % 2
        copy = pltpu.make_async_remote_copy(
            pgs.at[e_], pgr.at[y_, e_], gss.at[y_, e_], grs.at[y_, e_], device_id=(e_, y_), device_id_type=MESH
        )
        copy.wait_recv()
        copy.wait_send()
        return carry

    lax.fori_loop(1, total, settle, 0)
    pd_ref[...] = pgr[0] + pgr[1]

    def await_sent(ref, sem):
        pltpu.make_async_remote_copy(ref, ref, sem, rs.at[0, 0, 0, 0], device_id=partner, device_id_type=MESH).wait_send()

    wide = tok - quarter
    await_sent(G.at[0, 0, pl.ds(0, nz * wide + quarter), :], sa)
    await_sent(G.at[0, :, pl.ds(0, nz * wide + quarter), :], sb)
    await_sent(G.at[:, 0], sp)
    for k in range(nz):

        @pl.when(jnp.logical_and(zk[k] <= z, z < nz - 1))
        def _():
            await_sent(G.at[0, 0, pl.ds(0, wide + 4 * quarter), :], sz.at[0, zk[k]])

        @pl.when(jnp.logical_and(zk[k] >= z, z > 0))
        def _():
            await_sent(G.at[0, 0, pl.ds(0, wide + 4 * quarter), :], sz.at[1, zk[k]])

    for k in range(nz):
        rows = pl.ds(pl.multiple_of(zk[k] * 4 * slots, 16), 4 * slots)
        pltpu.make_async_copy(dhb.at[rows, :], dh_ref.at[rows, :], ds_.at[k]).wait()
    for n in range(8):
        dest = pl.ds(n * width, width)
        pltpu.make_async_copy(obuf.at[:, dest], gw_ref.at[:, dest], os_.at[n]).wait()


def fused_shards(grad_out, routes, scores, hidden_act, w_down):
    n_exp = lax.axis_size("expert")
    nz = n_exp // 4
    tok, feat = grad_out.shape
    slot_count, hid = hidden_act.shape[1:]
    slots = slot_count // n_exp
    experts = jnp.arange(n_exp, dtype=jnp.int32)
    gates = jax.nn.sigmoid(scores)
    gate_sum = jnp.sum(gates, axis=1, keepdims=True)
    probs = gates / gate_sum
    onehot = routes[None, :, :] == experts[:, None, None]
    dense = jnp.sum(jnp.where(onehot, probs[None], 0.0), axis=2)
    pm = jnp.broadcast_to(dense[:, None, :], (n_exp, 8, tok))
    bf, f32 = jnp.bfloat16, jnp.float32
    dma = pltpu.SemaphoreType.DMA
    d_hidden, grad_w, pd = pl.pallas_call(
        functools.partial(kernel, (nz, tok, feat, hid, slots)),
        out_shape=(
            jax.ShapeDtypeStruct((slot_count, hid), bf),
            jax.ShapeDtypeStruct((hid, 2 * feat), bf),
            jax.ShapeDtypeStruct((n_exp, 8, tok), f32),
        ),
        in_specs=[
            pl.BlockSpec(memory_space=pltpu.VMEM),
            pl.BlockSpec(memory_space=pl.ANY),
            pl.BlockSpec(memory_space=pl.ANY),
            pl.BlockSpec(memory_space=pl.ANY),
        ],
        out_specs=(
            pl.BlockSpec(memory_space=pl.ANY),
            pl.BlockSpec(memory_space=pl.ANY),
            pl.BlockSpec(memory_space=pltpu.VMEM),
        ),
        scratch_shapes=[
            pltpu.VMEM((nz, 2, 4 * tok, feat), bf),
            pltpu.VMEM((hid, 2 * feat), bf),
            pltpu.VMEM((slot_count, hid), bf),
            pltpu.VMEM((nz, hid, 4 * tok), bf),
            pltpu.VMEM((nz, hid, 4 * tok), bf),
            pltpu.VMEM((n_exp, slots, tok), bf),
            pltpu.VMEM((hid, 2 * feat), f32),
            pltpu.VMEM((hid, 2 * feat), bf),
            pltpu.VMEM((slot_count, hid), bf),
            pltpu.VMEM((hid, 2 * tok), f32),
            pltpu.VMEM((n_exp, 8, tok), f32),
            pltpu.VMEM((n_exp, 8, tok), f32),
            pltpu.VMEM((2, n_exp, 8, tok), f32),
            dma((nz, 4, 2, 2)),
            dma,
            dma,
            dma((2, nz)),
            dma,
            dma((n_exp,)),
            dma((n_exp,)),
            dma((2, n_exp)),
            dma((2, n_exp)),
            dma((3,)),
            dma((8,)),
            dma((nz,)),
        ],
        compiler_params=pltpu.CompilerParams(
            collective_id=0, has_side_effects=True, vmem_limit_bytes=VMEM_BYTES
        ),
    )(pm, grad_out, hidden_act[0], w_down[0])
    values = pd[:, 0, :]
    prob_grad = jnp.sum(jnp.where(onehot, values[:, :, None], 0.0), axis=0)
    mean_term = jnp.sum(probs * prob_grad, axis=1, keepdims=True)
    grad_scores = gates * (1.0 - gates) * (prob_grad - mean_term) / gate_sum
    return d_hidden[None], grad_w[None], grad_scores


def shards(grad_out, routes, scores, hidden_act, w_down):
    expert_count = lax.axis_size("expert")
    tok_rows = routes.shape[0]
    top_count = routes.shape[1]
    slot_count = hidden_act.shape[1]
    per_source = slot_count // expert_count
    flat_routes = routes.reshape(-1)
    onehot = (flat_routes[:, None] == jnp.arange(expert_count, dtype=jnp.int32)[None, :]).astype(
        jnp.int32
    )
    slot_rank = jnp.sum((jnp.cumsum(onehot, axis=0) - onehot) * onehot, axis=1)
    slot_place = flat_routes * per_source + slot_rank
    gates = jax.nn.sigmoid(scores)
    gate_sum = jnp.sum(gates, axis=1, keepdims=True)
    probs = gates / gate_sum
    token_ids = jnp.arange(tok_rows * top_count, dtype=jnp.int32) // top_count
    slot_owner = (
        jnp.full((expert_count * per_source,), tok_rows, jnp.int32).at[slot_place].set(token_ids)
    )
    slot_probs = (
        jnp.zeros((expert_count * per_source,), jnp.float32).at[slot_place].set(probs.reshape(-1))
    )
    saved_act = hidden_act[0]
    down_rows = w_down[0]
    outgoing = jnp.take(grad_out, slot_owner, axis=0, mode="fill", fill_value=0).reshape(
        expert_count, per_source, -1
    )
    narrow, slot_weight = (
        lax.all_to_all(outgoing, "expert", split_axis=0, concat_axis=0, tiled=True),
        lax.all_to_all(
            slot_probs.reshape(expert_count, per_source).astype(jnp.bfloat16),
            "expert",
            split_axis=0,
            concat_axis=0,
            tiled=True,
        ).astype(jnp.float32),
    )
    narrow = narrow.reshape(slot_count, -1)
    slot_weight = slot_weight.reshape(slot_count)
    segment = lax.all_gather(narrow, "tensor", axis=1, tiled=True)
    proj_sum = lax.dot_general(
        segment, down_rows, (((1,), (1,)), ((), ())), preferred_element_type=jnp.float32
    )
    scaled = (segment * slot_weight[:, None]).astype(jnp.bfloat16)
    fresh = lax.dot_general(
        saved_act, scaled, (((0,), (0,)), ((), ())), preferred_element_type=jnp.float32
    )
    partial_value = jnp.sum(proj_sum * saved_act.astype(jnp.float32), axis=1)
    hidden_grad = (slot_weight[:, None] * proj_sum).astype(jnp.bfloat16)
    summed = lax.psum(partial_value, "tensor")
    returned = lax.all_to_all(
        summed.reshape(expert_count, per_source), "expert", split_axis=0, concat_axis=0, tiled=True
    )
    prob_grad = returned.reshape(-1)[slot_place].reshape(tok_rows, top_count)
    mean_term = jnp.sum(probs * prob_grad, axis=1, keepdims=True)
    grad_scores = gates * (1.0 - gates) * (prob_grad - mean_term) / gate_sum
    return (hidden_grad[None], fresh.astype(jnp.bfloat16)[None], grad_scores)


def fits(mesh):
    return mesh.shape["tensor"] == 2 and mesh.shape["expert"] % 4 == 0 and mesh.shape["expert"] <= 16


def solution(mesh):
    return jax.shard_map(
        fused_shards if fits(mesh) else shards,
        mesh=mesh,
        in_specs=(
            P("expert", "tensor"),
            P("expert", None),
            P("expert", None),
            P("expert", None, "tensor"),
            P("expert", "tensor", None),
        ),
        out_specs=(P("expert", None, "tensor"), P("expert", "tensor", None), P("expert", None)),
        check_vma=False,
    )
```

```python
import functools

import jax
import jax.numpy as jnp
from jax import lax
from jax.experimental import pallas as pl
from jax.experimental.pallas import tpu as pltpu
from jax.sharding import PartitionSpec as P

MESH = pl.DeviceIdType.MESH
NT = (((1,), (1,)), ((), ()))
TN = (((0,), (0,)), ((), ()))
VMEM_BYTES = 57_000_000


def item_order(ranks):
    items = [(k, a, b) for k in range(ranks) for a in (0, 1) for b in (0, 1)]
    return sorted(items, key=lambda i: (i[0] + i[1] * 0.9 + i[2] * (1.2 + 0.5 * i[0] + 0.3 * i[1]), i))


def kernel(
    dims,
    routes_ref,
    scores_ref,
    g_ref,
    h_ref,
    w_ref,
    dhb,
    obuf,
    gs_ref,
    G,
    W,
    H,
    HT,
    HpT,
    sel,
    acc,
    dht,
    bpt,
    pm_ref,
    pr,
    pgs,
    pgr,
    rs,
    sa,
    sb,
    sz,
    sp,
    pss,
    prs,
    gss,
    grs,
    ls,
):
    nz, tok, feat, hid, slots = dims
    n_exp = nz * 4
    group = 4 * tok
    quarter = tok // 4
    pieces = ((0, tok - quarter, 1), (tok - quarter, quarter, 2))
    e = lax.axis_index("expert")
    y = lax.axis_index("tensor")
    z, x, c = e // 4, (e // 2) % 2, e % 2

    tables = [sorted(range(nz), key=lambda o: (abs(o - i), o)) for i in range(nz)]

    def ranked(k):
        val = jnp.int32(0)
        for i in range(nz):
            val = val + jnp.where(z == i, jnp.int32(tables[i][k]), jnp.int32(0))
        return val

    zk = [ranked(k) for k in range(nz)]

    def dev(z_, x_, y_, c_):
        return ((z_ * 2 + x_) * 2 + c_, y_)

    load_g = pltpu.make_async_copy(g_ref, G.at[z, y, pl.ds((x * 2 + c) * tok, tok), :], ls.at[0])
    load_h = pltpu.make_async_copy(h_ref, H, ls.at[1])
    load_w = pltpu.make_async_copy(w_ref, W, ls.at[2])
    load_g.start()
    load_h.start()
    load_w.start()

    barrier = pltpu.get_barrier_semaphore()
    total = n_exp * 2
    lin = e * 2 + y
    top = routes_ref.shape[0]
    choices = routes_ref[...]
    gates = jax.nn.sigmoid(scores_ref[...])
    gate_sum = jnp.sum(gates, axis=0, keepdims=True)
    probs = gates / gate_sum

    def greet(i, carry):
        to = (lin + i) % total
        pl.semaphore_signal(barrier, inc=1, device_id=(to // 2, to % 2), device_id_type=MESH)
        return carry

    lax.fori_loop(1, total, greet, 0)
    for ex in range(n_exp):
        row = jnp.sum(jnp.where(choices == ex, probs, 0.0), axis=0, keepdims=True)
        pm_ref[ex] = jnp.broadcast_to(row, (8, tok))
    pl.semaphore_wait(barrier, total - 1)

    partner = dev(z, x, y, 1 - c)
    a_dev = dev(z, (x + 1 - c) % 2, (y + c) % 2, c)
    b_dev = dev(z, (x + c) % 2, (y + 1 - c) % 2, c)
    up_dev = dev(jnp.minimum(z + 1, nz - 1), x, y, c)
    down_dev = dev(jnp.maximum(z - 1, 0), x, y, c)

    def place(k, a, b, color, piece):
        fx = a * (1 - color) + b * color
        fy = a * color + b * (1 - color)
        x_, y_ = (x + fx) % 2, (y + fy) % 2
        row, rows, _ = pieces[piece]
        ref = G.at[zk[k], y_, pl.ds((x_ * 2 + color) * tok + row, rows), :]
        return ref, rs.at[zk[k], x_ * 2 + color, y_, piece]

    def send(ref, recv, sem, to):
        pltpu.make_async_remote_copy(ref, ref, sem, recv, device_id=to, device_id_type=MESH).start()

    def await_piece(ref, recv):
        pltpu.make_async_remote_copy(ref, ref, sp, recv, device_id=partner, device_id_type=MESH).wait_recv()

    def handle(k, a, b):
        for piece in range(len(pieces)):
            kind = pieces[piece][2]
            ref, recv = place(k, a, b, c, piece)
            if (k, a, b) != (0, 0, 0):
                await_piece(ref, recv)
            if (a, b) == (0, 0) or kind == 2:

                @pl.when(jnp.logical_and(zk[k] <= z, z < nz - 1))
                def _():
                    send(ref, recv, sz.at[0, zk[k]], up_dev)

                @pl.when(jnp.logical_and(zk[k] >= z, z > 0))
                def _():
                    send(ref, recv, sz.at[1, zk[k]], down_dev)

            if (a, b) == (0, 0) and (kind == 1 or k == 0):
                send(ref, recv, sa, a_dev)
            if b == 0 and (kind == 1 or k == 0):
                send(ref, recv, sb, b_dev)
            send(ref, recv, sp, partner)

    load_g.wait()
    handle(0, 0, 0)

    def send_p(i, carry):
        to = (e + i) % n_exp
        pltpu.make_async_remote_copy(
            pm_ref.at[to], pr.at[e], pss.at[to], prs.at[e], device_id=(to, y), device_id_type=MESH
        ).start()
        return carry

    lax.fori_loop(1, n_exp, send_p, 0)
    pr[e] = pm_ref[e]

    def wait_p(i, carry):
        frm = (e + i) % n_exp
        copy = pltpu.make_async_remote_copy(
            pm_ref.at[frm], pr.at[frm], pss.at[frm], prs.at[frm], device_id=(frm, y), device_id_type=MESH
        )
        copy.wait_recv()
        copy.wait_send()
        return carry

    lax.fori_loop(1, n_exp, wait_p, 0)
    load_h.wait()
    before = (
        lax.broadcasted_iota(jnp.int32, (tok, tok), 0) < lax.broadcasted_iota(jnp.int32, (tok, tok), 1)
    ).astype(jnp.bfloat16)
    slot_ids = lax.broadcasted_iota(jnp.int32, (4 * slots, tok), 0).astype(jnp.float32)

    def prepare(line, carry):
        cols = pl.ds(pl.multiple_of(line * 4 * slots, 128), 4 * slots)
        for j in range(4):
            p = pr[line * 4 + j]
            routed = (p > 0.0).astype(jnp.float32)
            rank = jnp.dot(routed.astype(jnp.bfloat16), before, preferred_element_type=jnp.float32)
            rank = jnp.where(p > 0.0, rank + j * slots, -1.0)
            pick = (slot_ids == rank[0:1, :]).astype(jnp.float32).astype(jnp.bfloat16)
            sel[line, :, j * tok : (j + 1) * tok] = pick
            ht = jnp.dot(H[:, cols], pick, preferred_element_type=jnp.float32)
            HT[line, :, j * tok : (j + 1) * tok] = ht.astype(jnp.bfloat16)
            HpT[line, :, j * tok : (j + 1) * tok] = (ht * p[0:1, :]).astype(jnp.bfloat16)
        return carry

    lax.fori_loop(0, nz, prepare, 0)

    def await_partner(k):
        for a in (0, 1):
            for b in (0, 1):
                for piece in range(len(pieces)):
                    await_piece(*place(k, a, b, 1 - c, piece))

    def project(k, half):
        line = zk[k]
        cols = slice(half * 2 * tok, (half + 1) * 2 * tok)
        bpt[...] = lax.dot_general(
            W[:, :feat], G[line, 0, cols, :], NT, preferred_element_type=jnp.float32
        ) + lax.dot_general(W[:, feat:], G[line, 1, cols, :], NT, preferred_element_type=jnp.float32)
        for i in range(2):
            j = half * 2 + i
            block = line * 4 + j
            back = bpt[:, i * tok : (i + 1) * tok]
            value = jnp.sum(
                back * HT[line, :, j * tok : (j + 1) * tok].astype(jnp.float32), axis=0, keepdims=True
            )
            pgs[block] = jnp.broadcast_to(value, (8, tok))
            dht[:, j * tok : (j + 1) * tok] = (back * pr[block][0:1, :]).astype(jnp.bfloat16)

    def send_values(k):
        line = zk[k]
        for j in range(4):
            block = line * 4 + j
            for y_ in range(2):

                @pl.when(jnp.logical_or(block != e, y != y_))
                def _():
                    pltpu.make_async_remote_copy(
                        pgs.at[block],
                        pgr.at[y, e],
                        gss.at[y_, block],
                        grs.at[y, e],
                        device_id=(block, y_),
                        device_id_type=MESH,
                    ).start()

        cols = pl.ds(pl.multiple_of(line * 4 * slots, 128), 4 * slots)
        dhb[:, cols] = lax.dot_general(dht[...], sel[line], NT, preferred_element_type=jnp.float32).astype(jnp.bfloat16)

    width = feat // 4

    def weigh(k, half):
        line = zk[k]

        def one(n, carry):
            cols = pl.ds(pl.multiple_of(n * width, width), width)
            dest = pl.ds(pl.multiple_of(half * feat + n * width, width), width)
            part = jnp.dot(HpT[line], G[line, half, :, cols], preferred_element_type=jnp.float32)
            if k == 0:
                acc[:, dest] = part
            elif k < nz - 1:
                acc[:, dest] += part
            else:
                obuf[:, dest] = (acc[:, dest] + part).astype(jnp.bfloat16)
            return carry

        lax.fori_loop(0, 4, one, 0)

    units = []
    for k in range(nz):
        units.append((k, lambda k=k: (await_partner(k), project(k, 0))))
        units.append((k, lambda k=k: (project(k, 1), send_values(k))))
        units.append((k, lambda k=k: weigh(k, 0)))
        units.append((k, lambda k=k: weigh(k, 1)))

    order = item_order(nz)[1:]
    done = {k: 1 if k == 0 else 0 for k in range(nz)}
    started = False
    for item in order:
        handle(*item)
        done[item[0]] += 1
        if units and done[units[0][0]] == 4:
            if not started:
                load_w.wait()
                started = True
            units.pop(0)[1]()
    for _, unit in units:
        unit()

    pgr[y, e] = pgs[e]

    def settle(i, carry):
        at = (lin + i) % total
        e_, y_ = at // 2, at % 2
        copy = pltpu.make_async_remote_copy(
            pgs.at[e_], pgr.at[y_, e_], gss.at[y_, e_], grs.at[y_, e_], device_id=(e_, y_), device_id_type=MESH
        )
        copy.wait_recv()
        copy.wait_send()
        return carry

    lax.fori_loop(1, total, settle, 0)
    wanted = jnp.zeros((top, tok), jnp.float32)
    for ex in range(n_exp):
        wanted = wanted + jnp.where(choices == ex, (pgr[0, ex] + pgr[1, ex])[0:1, :], 0.0)
    mean_term = jnp.sum(probs * wanted, axis=0, keepdims=True)
    gs_ref[...] = gates * (1.0 - gates) * (wanted - mean_term) / gate_sum

    def await_sent(ref, sem):
        pltpu.make_async_remote_copy(ref, ref, sem, rs.at[0, 0, 0, 0], device_id=partner, device_id_type=MESH).wait_send()

    wide = tok - quarter
    await_sent(G.at[0, 0, pl.ds(0, nz * wide + quarter), :], sa)
    await_sent(G.at[0, :, pl.ds(0, nz * wide + quarter), :], sb)
    await_sent(G.at[:, 0], sp)
    for k in range(nz):

        @pl.when(jnp.logical_and(zk[k] <= z, z < nz - 1))
        def _():
            await_sent(G.at[0, 0, pl.ds(0, wide + 4 * quarter), :], sz.at[0, zk[k]])

        @pl.when(jnp.logical_and(zk[k] >= z, z > 0))
        def _():
            await_sent(G.at[0, 0, pl.ds(0, wide + 4 * quarter), :], sz.at[1, zk[k]])


def fused_shards(grad_out, routes, scores, hidden_act, w_down):
    n_exp = lax.axis_size("expert")
    nz = n_exp // 4
    tok, feat = grad_out.shape
    slot_count, hid = hidden_act.shape[1:]
    slots = slot_count // n_exp
    bf, f32 = jnp.bfloat16, jnp.float32
    dma = pltpu.SemaphoreType.DMA
    d_hidden, grad_w, grad_scores = pl.pallas_call(
        functools.partial(kernel, (nz, tok, feat, hid, slots)),
        out_shape=(
            pltpu.VMEM((hid, slot_count), bf),
            pltpu.VMEM((hid, 2 * feat), bf),
            jax.ShapeDtypeStruct(scores.shape[::-1], f32),
        ),
        in_specs=[
            pl.BlockSpec(memory_space=pltpu.VMEM),
            pl.BlockSpec(memory_space=pltpu.VMEM),
            pl.BlockSpec(memory_space=pl.ANY),
            pl.BlockSpec(memory_space=pl.ANY),
            pl.BlockSpec(memory_space=pl.ANY),
        ],
        out_specs=(
            pl.BlockSpec(memory_space=pltpu.VMEM),
            pl.BlockSpec(memory_space=pltpu.VMEM),
            pl.BlockSpec(memory_space=pltpu.VMEM),
        ),
        scratch_shapes=[
            pltpu.VMEM((nz, 2, 4 * tok, feat), bf),
            pltpu.VMEM((hid, 2 * feat), bf),
            pltpu.VMEM((hid, slot_count), bf),
            pltpu.VMEM((nz, hid, 4 * tok), bf),
            pltpu.VMEM((nz, hid, 4 * tok), bf),
            pltpu.VMEM((nz, 4 * slots, 4 * tok), bf),
            pltpu.VMEM((hid, 2 * feat), f32),
            pltpu.VMEM((hid, 4 * tok), bf),
            pltpu.VMEM((hid, 2 * tok), f32),
            pltpu.VMEM((n_exp, 8, tok), f32),
            pltpu.VMEM((n_exp, 8, tok), f32),
            pltpu.VMEM((n_exp, 8, tok), f32),
            pltpu.VMEM((2, n_exp, 8, tok), f32),
            dma((nz, 4, 2, 2)),
            dma,
            dma,
            dma((2, nz)),
            dma,
            dma((n_exp,)),
            dma((n_exp,)),
            dma((2, n_exp)),
            dma((2, n_exp)),
            dma((3,)),
        ],
        compiler_params=pltpu.CompilerParams(
            collective_id=0, has_side_effects=True, vmem_limit_bytes=VMEM_BYTES
        ),
    )(routes.T, scores.T, grad_out, hidden_act[0].T, w_down[0])
    return d_hidden.T[None], grad_w[None], grad_scores.T


def shards(grad_out, routes, scores, hidden_act, w_down):
    expert_count = lax.axis_size("expert")
    tok_rows = routes.shape[0]
    top_count = routes.shape[1]
    slot_count = hidden_act.shape[1]
    per_source = slot_count // expert_count
    flat_routes = routes.reshape(-1)
    onehot = (flat_routes[:, None] == jnp.arange(expert_count, dtype=jnp.int32)[None, :]).astype(
        jnp.int32
    )
    slot_rank = jnp.sum((jnp.cumsum(onehot, axis=0) - onehot) * onehot, axis=1)
    slot_place = flat_routes * per_source + slot_rank
    gates = jax.nn.sigmoid(scores)
    gate_sum = jnp.sum(gates, axis=1, keepdims=True)
    probs = gates / gate_sum
    token_ids = jnp.arange(tok_rows * top_count, dtype=jnp.int32) // top_count
    slot_owner = (
        jnp.full((expert_count * per_source,), tok_rows, jnp.int32).at[slot_place].set(token_ids)
    )
    slot_probs = (
        jnp.zeros((expert_count * per_source,), jnp.float32).at[slot_place].set(probs.reshape(-1))
    )
    saved_act = hidden_act[0]
    down_rows = w_down[0]
    outgoing = jnp.take(grad_out, slot_owner, axis=0, mode="fill", fill_value=0).reshape(
        expert_count, per_source, -1
    )
    narrow, slot_weight = (
        lax.all_to_all(outgoing, "expert", split_axis=0, concat_axis=0, tiled=True),
        lax.all_to_all(
            slot_probs.reshape(expert_count, per_source).astype(jnp.bfloat16),
            "expert",
            split_axis=0,
            concat_axis=0,
            tiled=True,
        ).astype(jnp.float32),
    )
    narrow = narrow.reshape(slot_count, -1)
    slot_weight = slot_weight.reshape(slot_count)
    segment = lax.all_gather(narrow, "tensor", axis=1, tiled=True)
    proj_sum = lax.dot_general(
        segment, down_rows, (((1,), (1,)), ((), ())), preferred_element_type=jnp.float32
    )
    scaled = (segment * slot_weight[:, None]).astype(jnp.bfloat16)
    fresh = lax.dot_general(
        saved_act, scaled, (((0,), (0,)), ((), ())), preferred_element_type=jnp.float32
    )
    partial_value = jnp.sum(proj_sum * saved_act.astype(jnp.float32), axis=1)
    hidden_grad = (slot_weight[:, None] * proj_sum).astype(jnp.bfloat16)
    summed = lax.psum(partial_value, "tensor")
    returned = lax.all_to_all(
        summed.reshape(expert_count, per_source), "expert", split_axis=0, concat_axis=0, tiled=True
    )
    prob_grad = returned.reshape(-1)[slot_place].reshape(tok_rows, top_count)
    mean_term = jnp.sum(probs * prob_grad, axis=1, keepdims=True)
    grad_scores = gates * (1.0 - gates) * (prob_grad - mean_term) / gate_sum
    return (hidden_grad[None], fresh.astype(jnp.bfloat16)[None], grad_scores)


def fits(mesh):
    return mesh.shape["tensor"] == 2 and mesh.shape["expert"] % 4 == 0 and mesh.shape["expert"] <= 16


def solution(mesh):
    return jax.shard_map(
        fused_shards if fits(mesh) else shards,
        mesh=mesh,
        in_specs=(
            P("expert", "tensor"),
            P("expert", None),
            P("expert", None),
            P("expert", None, "tensor"),
            P("expert", "tensor", None),
        ),
        out_specs=(P("expert", None, "tensor"), P("expert", "tensor", None), P("expert", None)),
        check_vma=False,
    )
```
